32 devices in a mesh: dp: 4 (over x, core), cp: 2 (over y), sp: 4 (over z).
Axes of the slice: x: 2, y: 2, z: 4, core: 2. Of those that a mesh axis runs over, the one named last changes fastest.
Arguments:
- hidden_in: bfloat16 [12, 1024, 1536], P('dp', ('cp', 'sp')), may hold values from -6 to 6
- doc_ids: int32 [12, 1024], P('dp', ('cp', 'sp')), may hold values from 0 to 3, as said below
- span_order: int32 [4], replicated, may hold values from 0 to 3, as said below
- norm1_gain: bfloat16 [1536], P(('dp', 'cp')), may hold values from 0.5 to 1.5
- w_query: bfloat16 [1536, 1536], P(('dp', 'cp')), may hold values from -0.15625 to 0.15625
- w_key: bfloat16 [1536, 768], P(('dp', 'cp')), may hold values from -0.15625 to 0.15625
- w_value: bfloat16 [1536, 768], P(('dp', 'cp')), may hold values from -0.15625 to 0.15625
- w_out: bfloat16 [1536, 1536], P(('dp', 'cp')), may hold values from -1.25 to 1.25
- norm2_gain: bfloat16 [1536], P(('dp', 'cp')), may hold values from 0.5 to 1.5
- w_gate: bfloat16 [1536, 4096], P(('dp', 'cp')), may hold values from -0.15625 to 0.15625
- w_up: bfloat16 [1536, 4096], P(('dp', 'cp')), may hold values from -0.15625 to 0.15625
- w_down: bfloat16 [4096, 1536], P(('dp', 'cp')), may hold values from -0.09375 to 0.09375
- out_cotangent: bfloat16 [12, 1024, 1536], P('dp', ('cp', 'sp')), may hold values from -6 to 6
Outputs:
- output: bfloat16 [12, 1024, 1536], P('dp', ('cp', 'sp'))
- d_hidden: bfloat16 [12, 1024, 1536], P('dp', ('cp', 'sp'))
- d_norm1_gain: float32 [1536], P(('dp', 'cp'))
- d_w_query: float32 [1536, 1536], P(('dp', 'cp'))
- d_w_key: float32 [1536, 768], P(('dp', 'cp'))
- d_w_value: float32 [1536, 768], P(('dp', 'cp'))
- d_w_out: float32 [1536, 1536], P(('dp', 'cp'))
- d_norm2_gain: float32 [1536], P(('dp', 'cp'))
- d_w_gate: float32 [1536, 4096], P(('dp', 'cp'))
- d_w_up: float32 [1536, 4096], P(('dp', 'cp'))
- d_w_down: float32 [4096, 1536], P(('dp', 'cp'))
The draws below stay inside these ranges and needn't reach their ends.
Inputs may be any that keep to these rules, and one draw needn't show every extreme that they name: `span_order`: a permutation in which device i of cp stores blocks 2i and 2i + 1 of each of its sequences, and these hold the positions j and 3 - j for some j, in either order; each j once. `doc_ids`: each sequence holds exactly 4 documents; in order of position within a sequence the numbers start at 0 and never fall.
All inputs are finite; a program needn't handle non-finite values.
Results may differ from the reference program's by a relative error of at most 0.014.
Values may be sent and summed in bfloat16 or wider, within the bound.
No kernel may reach another device: no remote copies, remote signals or barrier semaphores. Data moves between devices by JAX's collectives and lax.ppermute only.
A program may use at most 256 MiB of HBM per device.

```python
import jax
import jax.numpy as jnp
from jax import lax

D = 1536
HEADS = 16
KV_HEADS = 8
HEAD_DIM = 96
FF = 4096
LEN = 1024
NCH = 4
SPAN = 256
BATCH = 12


def span_table(key):
    half_count = NCH // 2
    pairing = jax.random.permutation(jax.random.fold_in(key, 101), half_count).astype(jnp.int32)
    flips = jax.random.randint(jax.random.fold_in(key, 102), (half_count,), 0, 2).astype(jnp.int32)
    mirror = (NCH - 1 - pairing).astype(jnp.int32)
    first_block = jnp.where(flips == 1, mirror, pairing)
    second_block = jnp.where(flips == 1, pairing, mirror)
    return jnp.stack((first_block, second_block), axis=1).reshape(NCH).astype(jnp.int32)


def draw_span_order(key, part):
    return span_table(key)


def draw_doc_ids(key, part):
    order = span_table(key)
    row_keys = jax.random.split(jax.random.fold_in(key, 202), BATCH)
    boundaries = jax.vmap(lambda row_key: jax.random.permutation(row_key, LEN - 1)[:3] + 1)(row_keys).astype(jnp.int32)
    positions = jnp.arange(LEN, dtype=jnp.int32)
    starts = jnp.sum((positions[None, :, None] == boundaries[:, None, :]).astype(jnp.int32), axis=2)
    orig_ids = jnp.cumsum(starts, axis=1).astype(jnp.int32)
    blocks = orig_ids.reshape(BATCH, NCH, SPAN)
    return jnp.take(blocks, order, axis=1).reshape(BATCH, LEN).astype(jnp.int32)


def block_scale(stream_key, extent, pieces, low, top_value):
    level = 1.0
    for position, parts in pieces:
        draws = jax.random.uniform(jax.random.fold_in(jax.random.fold_in(stream_key, 6), position), (parts,), jnp.float32, low / len(pieces), top_value / len(pieces))
        level = level * jnp.repeat(jnp.exp(draws), extent[position] // parts).reshape((-1,) + (1,) * (len(extent) - 1 - position))
    return level


def gaussian(own_key, shape, spread, limit, cuts=(), held_as=jnp.bfloat16):
    values = spread * jax.random.normal(own_key, shape, jnp.float32)
    if cuts:
        values = values * block_scale(own_key, shape, cuts, -0.22, 0.18)
    return jnp.clip(values, -limit, limit).astype(held_as)


def setup_inputs(seed: int = 0) -> dict:
    splits = jax.random.split(jax.random.key(seed), 14)
    hidden_in = gaussian(splits[0], (BATCH, LEN, D), 1.0, 6.0, ((0, 4), (1, 8)))
    doc_ids = draw_doc_ids(jax.random.fold_in(splits[13], 71), 0)
    span_order = draw_span_order(jax.random.fold_in(splits[13], 71), 0)
    norm1_gain = jnp.clip(1.0 + 0.1 * jax.random.normal(splits[3], (D,), jnp.float32), 0.5, 1.5).astype(jnp.bfloat16)
    w_query = gaussian(splits[4], (D, HEADS * HEAD_DIM), D ** -0.5, 0.15625, ((0, 8),))
    w_key = gaussian(splits[5], (D, KV_HEADS * HEAD_DIM), D ** -0.5, 0.15625, ((0, 8),))
    w_value = gaussian(splits[6], (D, KV_HEADS * HEAD_DIM), D ** -0.5, 0.15625, ((0, 8),))
    w_out = gaussian(splits[7], (HEADS * HEAD_DIM, D), (D // 64) ** -0.5, 1.25, ((0, 8),))
    norm2_gain = jnp.clip(1.0 + 0.1 * jax.random.normal(splits[8], (D,), jnp.float32), 0.5, 1.5).astype(jnp.bfloat16)
    w_gate = gaussian(splits[9], (D, FF), D ** -0.5, 0.15625, ((0, 8),))
    w_up = gaussian(splits[10], (D, FF), D ** -0.5, 0.15625, ((0, 8),))
    w_down = gaussian(splits[11], (FF, D), FF ** -0.5, 0.09375, ((0, 8),))
    out_cotangent = gaussian(splits[12], (BATCH, LEN, D), 1.0, 6.0, ((0, 4), (1, 8)))
    return dict(hidden_in=hidden_in, doc_ids=doc_ids, span_order=span_order, norm1_gain=norm1_gain, w_query=w_query, w_key=w_key, w_value=w_value, w_out=w_out, norm2_gain=norm2_gain, w_gate=w_gate, w_up=w_up, w_down=w_down, out_cotangent=out_cotangent)


EPSILON = 1e-05
ROPE_BASE = 100000.0

@jax.custom_vjp
def low(v):
    return lax.optimization_barrier(v.astype(jnp.bfloat16)).astype(jnp.float32)

@jax.custom_vjp
def low_back(v):
    return v

def low_keep(v):
    return (low(v), None)

def low_pass(kept, grad):
    return (grad,)

def back_keep(v):
    return (v, None)

def back_low(kept, grad):
    return (low(grad),)
low.defvjp(low_keep, low_pass)
low_back.defvjp(back_keep, back_low)

def rope_tables(positions, head_dim):
    half_dim = head_dim // 2
    frequency = ROPE_BASE ** (-(jnp.arange(half_dim, dtype=jnp.float32) * 2.0 / head_dim))
    angles = positions.astype(jnp.float32)[..., None] * frequency
    return (jnp.cos(angles), jnp.sin(angles))

def rotate(values, cosine_table, sine_table):
    half_dim = values.shape[-1] // 2
    first_half = values[..., :half_dim]
    second_half = values[..., half_dim:]
    cosine_b = cosine_table[..., None, :]
    sine_b = sine_table[..., None, :]
    return jnp.concatenate([first_half * cosine_b - second_half * sine_b, second_half * cosine_b + first_half * sine_b], axis=-1)

def initial_positions(stored, span_order, span_rows):
    span_index = stored // span_rows
    match_table = span_index[:, None] == jnp.arange(span_order.shape[0], dtype=jnp.int32)[None, :]
    picked = lax.optimization_barrier(jnp.sum(jnp.where(match_table, span_order[None, :], 0), axis=1)).astype(jnp.int32)
    return (picked * span_rows + stored % span_rows).astype(jnp.int32)

def matmul(left, right, form):
    return jnp.einsum(form, left, right, precision=lax.Precision.HIGHEST)

def rms_apply(values, gain_vec):
    return values * lax.rsqrt(lax.optimization_barrier(jnp.mean(values * values, axis=-1, keepdims=True)) + EPSILON) * gain_vec

def reference(hidden_in, doc_ids, span_order, norm1_gain, w_query, w_key, w_value, w_out, norm2_gain, w_gate, w_up, w_down, out_cotangent):
    group_size = HEADS // KV_HEADS
    block_rows = min(512, LEN)
    block_count = LEN // block_rows
    factor = HEAD_DIM ** (-0.5)
    key_orig = initial_positions(jnp.arange(LEN, dtype=jnp.int32), span_order, SPAN)
    cosine_table, sine_table = rope_tables(key_orig, HEAD_DIM)

    def attend_block(query_block, keys_rep, values_rep, doc_block, orig_block, doc_row):
        raw_scores = matmul(query_block, keys_rep, 'qhd,khd->hqk') * factor
        raw_scores = low_back(raw_scores)
        allowed = (doc_block[:, None] == doc_row[None, :]) & (key_orig[None, :] <= orig_block[:, None])
        masked_scores = jnp.where(allowed[None], raw_scores, -1e+30)
        row_max = lax.optimization_barrier(jnp.max(masked_scores, axis=-1, keepdims=True))
        log_total = row_max + jnp.log(lax.optimization_barrier(jnp.sum(jnp.exp(masked_scores - row_max), axis=-1, keepdims=True)))
        probability = low(jnp.exp(masked_scores - log_total))
        return matmul(probability, values_rep, 'hqk,khd->qhd')
    attend = jax.checkpoint(attend_block)

    def layer(hidden, doc_row, params):
        gain_one, query_w, key_w, value_w, out_w, gain_two, gate_w, up_w, down_w = params
        normed = low(rms_apply(hidden, gain_one))
        query = low(rotate(low_back(matmul(normed, query_w, 'td,dk->tk')).reshape(LEN, HEADS, HEAD_DIM), cosine_table, sine_table))
        keys = low(rotate(low_back(matmul(normed, key_w, 'td,dk->tk')).reshape(LEN, KV_HEADS, HEAD_DIM), cosine_table, sine_table))
        values = low(low_back(matmul(normed, value_w, 'td,dk->tk'))).reshape(LEN, KV_HEADS, HEAD_DIM)
        keys_rep = jnp.repeat(keys, group_size, axis=1)
        values_rep = jnp.repeat(values, group_size, axis=1)
        query_blocks = query.reshape(block_count, block_rows, HEADS, HEAD_DIM)
        attended = lax.map(lambda bundle: attend(bundle[0], keys_rep, values_rep, bundle[1], bundle[2], doc_row), (query_blocks, doc_row.reshape(block_count, block_rows), key_orig.reshape(block_count, block_rows)))
        attended = low(low_back(attended.reshape(LEN, HEADS * HEAD_DIM)))
        middle = hidden + low_back(matmul(attended, out_w, 'tk,kd->td'))
        normed_two = low(rms_apply(middle, gain_two))
        gate_proj = low_back(matmul(normed_two, gate_w, 'td,df->tf'))
        up_proj = low_back(matmul(normed_two, up_w, 'td,df->tf'))
        hidden_ff = low(jax.nn.silu(gate_proj) * up_proj)
        return middle + low_back(matmul(hidden_ff, down_w, 'tf,fd->td'))
    params = tuple((weight_arr.astype(jnp.float32) for weight_arr in (norm1_gain, w_query, w_key, w_value, w_out, norm2_gain, w_gate, w_up, w_down)))
    zero_grads = tuple((jnp.zeros(weight_arr.shape, jnp.float32) for weight_arr in params))

    def step(totals, bundle):
        hidden, doc_row, cotangent = bundle

        def apply(hidden_val, *param_vals):
            return layer(hidden_val, doc_row, param_vals)
        result, pullback = jax.vjp(apply, hidden.astype(jnp.float32), *params)
        grads = pullback(cotangent.astype(jnp.float32))
        totals = tuple((total_g + part_g for total_g, part_g in zip(totals, grads[1:])))
        return (totals, (result.astype(jnp.bfloat16), grads[0].astype(jnp.bfloat16)))
    totals, (outputs, d_inputs) = lax.scan(step, zero_grads, (hidden_in, doc_ids, out_cotangent))
    return (outputs, d_inputs, totals[0], totals[1], totals[2], totals[3], totals[4], totals[5], totals[6], totals[7], totals[8])
```

```python
import functools

import jax
import jax.numpy as jnp
import numpy as np
from jax import lax
from jax.experimental import pallas as pl
from jax.experimental.pallas import tpu as pltpu
from jax.sharding import PartitionSpec as P

HEAD_DIM = 96
HALF = HEAD_DIM // 2
PAD = 128
EPSILON = 1e-05
ROPE_BASE = 100000.0
LOG2E = 1.4426950408889634
BF = jnp.bfloat16
F32 = jnp.float32


def flip(value, axis, bit):
    n = lax.axis_size(axis)
    return lax.ppermute(value, axis, [(i, i ^ bit) for i in range(n)])


def shift(value, axis, by):
    n = lax.axis_size(axis)
    return lax.ppermute(value, axis, [(i, (i + by) % n) for i in range(n)])


def bit_set(axis, bit):
    return (lax.axis_index(axis) & bit) != 0


def cat(arrays, axis):
    return arrays[0] if len(arrays) == 1 else jnp.concatenate(arrays, axis=axis)


def bits_of(n):
    return [1 << b for b in reversed(range(n.bit_length() - 1))]


def gather_bit(pieces, axis, bit, pos):
    hi = bit_set(axis, bit)
    keys = sorted(pieces)
    rows = pieces[keys[0]].shape[0]
    got = flip(cat([pieces[k] for k in keys], 0), axis, bit)
    out = {}
    for i, k in enumerate(keys):
        mine, recv = pieces[k], got[i * rows : (i + 1) * rows]
        for b in (0, 1):
            new = list(k)
            new[pos] = b
            out[tuple(new)] = jnp.where(hi, mine, recv) if b else jnp.where(hi, recv, mine)
    return out


def reduce_bit(pieces, axis, bit, pos):
    hi = bit_set(axis, bit)
    keys = sorted(k for k in pieces if k[pos] == 0)
    mine, send = {}, []
    for k in keys:
        top = k[:pos] + (1,) + k[pos + 1 :]
        mine[k] = jnp.where(hi, pieces[top], pieces[k])
        send.append(jnp.where(hi, pieces[k], pieces[top]))
    rows = send[0].shape[0]
    got = flip(cat([s.astype(BF) for s in send], 0), axis, bit)
    return {k: mine[k].astype(F32) + got[i * rows : (i + 1) * rows].astype(F32) for i, k in enumerate(keys)}


def split_rows(value, shape):
    count = int(np.prod(shape))
    rows = value.shape[0] // count
    return {k: value[i * rows : (i + 1) * rows] for i, k in enumerate(np.ndindex(*shape))}


def join_rows(pieces):
    return cat([pieces[k] for k in sorted(pieces)], 0)


def swap_bit(grid, axis, bit, rpos, cpos):
    hi = bit_set(axis, bit)
    rks = sorted({r for r, _ in grid})
    cks = sorted({c for _, c in grid if c[cpos] == 0})
    up = lambda c: c[:cpos] + (1,) + c[cpos + 1 :]
    mine = {(r, c): jnp.where(hi, grid[r, up(c)], grid[r, c]) for r in rks for c in cks}
    send = cat([cat([jnp.where(hi, grid[r, c], grid[r, up(c)]) for c in cks], 1) for r in rks], 0)
    got = flip(send, axis, bit)
    h, w = mine[rks[0], cks[0]].shape
    out = {}
    for i, r in enumerate(rks):
        for j, c in enumerate(cks):
            recv = got[i * h : (i + 1) * h, j * w : (j + 1) * w]
            for b in (0, 1):
                new = r[:rpos] + (b,) + r[rpos + 1 :]
                out[new, c] = jnp.where(hi, mine[r, c], recv) if b else jnp.where(hi, recv, mine[r, c])
    return out


def unswap_bit(grid, axis, bit, rpos, cpos):
    hi = bit_set(axis, bit)
    rks = sorted({r for r, _ in grid if r[rpos] == 0})
    cks = sorted({c for _, c in grid})
    up = lambda r: r[:rpos] + (1,) + r[rpos + 1 :]
    mine = {(r, c): jnp.where(hi, grid[up(r), c], grid[r, c]) for r in rks for c in cks}
    send = cat([cat([jnp.where(hi, grid[r, c], grid[up(r), c]) for c in cks], 1) for r in rks], 0)
    got = flip(send, axis, bit)
    h, w = mine[rks[0], cks[0]].shape
    out = {}
    for i, r in enumerate(rks):
        for j, c in enumerate(cks):
            recv = got[i * h : (i + 1) * h, j * w : (j + 1) * w]
            for b in (0, 1):
                new = c[:cpos] + (b,) + c[cpos + 1 :]
                out[r, new] = jnp.where(hi, mine[r, c], recv) if b else jnp.where(hi, recv, mine[r, c])
    return out


def sum_sp(value):
    n = lax.axis_size("sp")
    if n != 4:
        return lax.psum(value.astype(F32), "sp").astype(BF).astype(F32)
    low = value.astype(BF)
    first = lax.ppermute(low, "sp", [(0, 1), (3, 2)])
    part = (value.astype(F32) + first.astype(F32)).astype(BF)
    second = lax.ppermute(part, "sp", [(1, 2), (2, 1)])
    total = (part.astype(F32) + second.astype(F32)).astype(BF)
    third = lax.ppermute(total, "sp", [(1, 0), (2, 3)])
    k = lax.axis_index("sp")
    return jnp.where((k == 0) | (k == 3), third, total).astype(F32)


def pick(pieces, index):
    return lax.select_n(index, *pieces) if len(pieces) > 1 else pieces[0]


def spread_matrix(heads):
    out = np.zeros((heads * HEAD_DIM, heads * PAD), np.float32)
    for h in range(heads):
        for i in range(HEAD_DIM):
            out[h * HEAD_DIM + i, h * PAD + (i // HALF) * (PAD // 2) + i % HALF] = 1.0
    return out


def dot(a, b, ca, cb):
    return lax.dot_general(a, b, (((ca,), (cb,)), ((), ())), preferred_element_type=F32)


def project_kernel(seqs, q_heads, kv_heads, n_ref, w_ref, cos_ref, sin_ref, sel_q_ref, sel_kv_ref, q_ref, kv_ref):
    x = n_ref[...]
    cos = jnp.concatenate([cos_ref[...]] * seqs, axis=0)
    sin = jnp.concatenate([sin_ref[...]] * seqs, axis=0)
    scale = HEAD_DIM ** (-0.5) * LOG2E

    def head(h):
        return dot(x, w_ref[:, h * PAD : (h + 1) * PAD], 1, 0)

    def turned(y):
        return y * cos + pltpu.roll(y, PAD // 2, 1) * sin

    q = jnp.concatenate([(turned(head(h)) * scale).astype(BF) for h in range(q_heads)], axis=1)
    q_ref[...] = dot(q, sel_q_ref[...], 1, 1).astype(BF)
    kv = jnp.concatenate(
        [turned(head(q_heads + h)).astype(BF) for h in range(kv_heads)]
        + [head(q_heads + kv_heads + h).astype(BF) for h in range(kv_heads)],
        axis=1,
    )
    kv_ref[...] = dot(kv, sel_kv_ref[...], 1, 1).astype(BF)


def fill_bias(bias_ref, codes_k, codes_q, floor_q):
    column = jnp.transpose(jnp.broadcast_to(codes_k, (PAD, codes_k.shape[1])))
    for j in range(codes_q.shape[1] // PAD):
        span = slice(j * PAD, (j + 1) * PAD)
        seen = (column <= codes_q[:, span]) & (column >= floor_q[:, span])
        bias_ref[:, span] = jnp.where(seen, 0.0, -1e30)


def attend_kernel(cfg, *refs):
    q_heads, kv_heads, nq, nk, chunk = cfg
    group = q_heads // kv_heads
    q_refs, refs = refs[:nq], refs[nq:]
    kv_refs, refs = refs[:nk], refs[nk:]
    codes_k, codes_q, floor_q, sel_q, sel_kv = refs[:5]
    refs = refs[5:]
    o_refs, lse_ref = refs[:nq], refs[nq]
    q_s, k_s, vt_s, bias_s, o_s = refs[nq + 1 :]
    rows = q_refs[0].shape[0]
    q_rows = nq * rows
    fill_bias(bias_s, codes_k[0], codes_q[0], floor_q[0])
    q_all = jnp.concatenate([r[...] for r in q_refs], axis=0)
    kv_all = jnp.concatenate([r[...] for r in kv_refs], axis=0)
    for h in range(q_heads):
        q_s[h] = dot(q_all, sel_q[:, h * PAD : (h + 1) * PAD], 1, 0).astype(BF)
    for h in range(kv_heads):
        k_s[h] = dot(kv_all, sel_kv[:, h * PAD : (h + 1) * PAD], 1, 0).astype(BF)
        vh = kv_heads + h
        vt_s[h] = dot(sel_kv[:, vh * PAD : (vh + 1) * PAD], kv_all, 0, 1).astype(BF)
    per = q_rows // chunk

    def step(i, carry):
        h = i // per
        at = pl.multiple_of((i % per) * chunk, chunk)
        kh = h // group
        s = dot(k_s[kh], q_s[h, pl.ds(at, chunk), :], 1, 1) + bias_s[:, pl.ds(at, chunk)]
        top = jnp.max(s, axis=0, keepdims=True)
        e = jnp.exp2(s - top)
        total = jnp.sum(e, axis=0, keepdims=True)
        o = dot(vt_s[kh], e.astype(BF), 1, 0) / total
        o_s[pl.ds(at, chunk), pl.ds(pl.multiple_of(h * PAD, PAD), PAD)] = jnp.transpose(o).astype(BF)
        lse_ref[0, pl.ds(h, 1), pl.ds(at, chunk)] = top + jnp.log2(total)
        return carry

    lax.fori_loop(0, q_heads * per, step, 0)
    o = dot(o_s[...], sel_q[...], 1, 1).astype(BF)
    for r in range(nq):
        o_refs[r][...] = o[r * rows : (r + 1) * rows]


def attend_back_kernel(cfg, *refs):
    q_heads, kv_heads, nq, nk, chunk = cfg
    group = q_heads // kv_heads
    q_refs, refs = refs[:nq], refs[nq:]
    do_refs, refs = refs[:nq], refs[nq:]
    kv_refs, refs = refs[:nk], refs[nk:]
    codes_k, codes_q, floor_q, sel_q, sel_kv, lse_ref, cos_q, sin_q, cos_k, sin_k = refs[:10]
    refs = refs[10:]
    dq_refs, dkv_refs = refs[:nq], refs[nq : nq + nk]
    q_s, do_s, k_s, kt_s, v_s, bias_s, dq_s, dk_s, dv_s = refs[nq + nk :]
    rows = q_refs[0].shape[0]
    q_rows = nq * rows
    fill_bias(bias_s, codes_k[0], codes_q[0], floor_q[0])
    q_all = jnp.concatenate([r[...] for r in q_refs], axis=0)
    do_all = jnp.concatenate([r[...] for r in do_refs], axis=0)
    kv_all = jnp.concatenate([r[...] for r in kv_refs], axis=0)
    for h in range(q_heads):
        span = slice(h * PAD, (h + 1) * PAD)
        q_s[h] = dot(q_all, sel_q[:, span], 1, 0).astype(BF)
        do_s[h] = dot(do_all, sel_q[:, span], 1, 0).astype(BF)
    for h in range(kv_heads):
        vh = kv_heads + h
        k_s[h] = dot(kv_all, sel_kv[:, h * PAD : (h + 1) * PAD], 1, 0).astype(BF)
        kt_s[h] = dot(sel_kv[:, h * PAD : (h + 1) * PAD], kv_all, 0, 1).astype(BF)
        v_s[h] = dot(kv_all, sel_kv[:, vh * PAD : (vh + 1) * PAD], 1, 0).astype(BF)
    dk_s[...] = jnp.zeros_like(dk_s)
    dv_s[...] = jnp.zeros_like(dv_s)
    per = q_rows // chunk

    def step(i, carry):
        h = i // per
        at = pl.multiple_of((i % per) * chunk, chunk)
        kh = h // group
        q = q_s[h, pl.ds(at, chunk), :]
        do = do_s[h, pl.ds(at, chunk), :]
        s = dot(k_s[kh], q, 1, 1) + bias_s[:, pl.ds(at, chunk)]
        p = jnp.exp2(s - lse_ref[0, pl.ds(h, 1), pl.ds(at, chunk)])
        dp = dot(v_s[kh], do, 1, 1)
        delta = jnp.sum(p * dp, axis=0, keepdims=True)
        ds = (p * (dp - delta)).astype(BF)
        dv_s[kh] += dot(p.astype(BF), do, 1, 0)
        dk_s[kh] += dot(ds, q, 1, 0)
        dq = dot(kt_s[kh], ds, 1, 0) * (HEAD_DIM ** (-0.5))
        swapped = jnp.concatenate([dq[PAD // 2 :], dq[: PAD // 2]], axis=0)
        dq = dq * cos_q[:, pl.ds(at, chunk)] + swapped * sin_q[:, pl.ds(at, chunk)]
        dq_s[pl.ds(at, chunk), pl.ds(pl.multiple_of(h * PAD, PAD), PAD)] = jnp.transpose(dq).astype(BF)
        return carry

    lax.fori_loop(0, q_heads * per, step, 0)
    dq = dot(dq_s[...], sel_q[...], 1, 1).astype(BF)
    for r in range(nq):
        dq_refs[r][...] = dq[r * rows : (r + 1) * rows]
    parts = []
    for h in range(kv_heads):
        dk = dk_s[h] * (1.0 / LOG2E)
        parts.append((dk * cos_k[...] - pltpu.roll(dk, PAD // 2, 1) * sin_k[...]).astype(BF))
    for h in range(kv_heads):
        parts.append(dv_s[h].astype(BF))
    dkv = dot(jnp.concatenate(parts, axis=1), sel_kv[...], 1, 1).astype(BF)
    for r in range(nk):
        dkv_refs[r][...] = dkv[r * rows : (r + 1) * rows]


VMEM_LIMIT = 60 << 20


def whole(shape):
    return pl.BlockSpec(shape, lambda *_: (0,) * len(shape))


def project(n_block, w_pad, cos, sin, sel_q, sel_kv, seqs, q_heads, kv_heads):
    rows, model = n_block.shape
    shapes = [
        jax.ShapeDtypeStruct((rows, q_heads * HEAD_DIM), BF),
        jax.ShapeDtypeStruct((rows, 2 * kv_heads * HEAD_DIM), BF),
    ]
    return pl.pallas_call(
        functools.partial(project_kernel, seqs, q_heads, kv_heads),
        out_shape=shapes,
        compiler_params=pltpu.CompilerParams(vmem_limit_bytes=VMEM_LIMIT),
        cost_estimate=pl.CostEstimate(
            flops=2 * rows * model * w_pad.shape[1],
            bytes_accessed=2 * (rows * model + model * w_pad.shape[1]),
            transcendentals=0,
        ),
        name="project",
    )(n_block, w_pad, cos, sin, sel_q, sel_kv)


def attend(qs, kvs, codes_k, codes_q, floor_q, sel_q, sel_kv, seqs, q_heads, kv_heads):
    nq, nk = len(qs), len(kvs)
    rows = qs[0].shape[0] // seqs
    qw, kw = qs[0].shape[1], kvs[0].shape[1]
    q_rows, k_rows = nq * rows, nk * rows
    chunk = min(256, q_rows)
    row = lambda n: pl.BlockSpec((1, 1, n), lambda s: (s, 0, 0))
    block = lambda w: pl.BlockSpec((rows, w), lambda s: (s, 0))
    flops = 4 * seqs * q_heads * q_rows * k_rows * PAD
    return pl.pallas_call(
        functools.partial(attend_kernel, (q_heads, kv_heads, nq, nk, chunk)),
        grid=(seqs,),
        in_specs=[block(qw)] * nq
        + [block(kw)] * nk
        + [row(k_rows), row(q_rows), row(q_rows), whole(sel_q.shape), whole(sel_kv.shape)],
        out_specs=[block(qw)] * nq + [pl.BlockSpec((1, q_heads, q_rows), lambda s: (s, 0, 0))],
        out_shape=[jax.ShapeDtypeStruct(q.shape, BF) for q in qs]
        + [jax.ShapeDtypeStruct((seqs, q_heads, q_rows), F32)],
        scratch_shapes=[
            pltpu.VMEM((q_heads, q_rows, PAD), BF),
            pltpu.VMEM((kv_heads, k_rows, PAD), BF),
            pltpu.VMEM((kv_heads, PAD, k_rows), BF),
            pltpu.VMEM((k_rows, q_rows), F32),
            pltpu.VMEM((q_rows, q_heads * PAD), BF),
        ],
        compiler_params=pltpu.CompilerParams(vmem_limit_bytes=VMEM_LIMIT),
        cost_estimate=pl.CostEstimate(
            flops=3 * flops, bytes_accessed=4 * seqs * (q_rows * qw + k_rows * kw), transcendentals=0
        ),
        name="attend",
    )(*qs, *kvs, codes_k, codes_q, floor_q, sel_q, sel_kv)


def attend_back(qs, dos, kvs, codes_k, codes_q, floor_q, sel_q, sel_kv, lse, tables, seqs, q_heads, kv_heads):
    nq, nk = len(qs), len(kvs)
    rows = qs[0].shape[0] // seqs
    qw, kw = qs[0].shape[1], kvs[0].shape[1]
    q_rows, k_rows = nq * rows, nk * rows
    chunk = min(256, q_rows)
    row = lambda n: pl.BlockSpec((1, 1, n), lambda s: (s, 0, 0))
    block = lambda w: pl.BlockSpec((rows, w), lambda s: (s, 0))
    flops = 10 * seqs * q_heads * q_rows * k_rows * PAD
    return pl.pallas_call(
        functools.partial(attend_back_kernel, (q_heads, kv_heads, nq, nk, chunk)),
        grid=(seqs,),
        in_specs=[block(qw)] * (2 * nq)
        + [block(kw)] * nk
        + [row(k_rows), row(q_rows), row(q_rows), whole(sel_q.shape), whole(sel_kv.shape)]
        + [pl.BlockSpec((1, q_heads, q_rows), lambda s: (s, 0, 0))]
        + [whole(t.shape) for t in tables],
        out_specs=[block(qw)] * nq + [block(kw)] * nk,
        out_shape=[jax.ShapeDtypeStruct(q.shape, BF) for q in qs] + [jax.ShapeDtypeStruct(k.shape, BF) for k in kvs],
        scratch_shapes=[
            pltpu.VMEM((q_heads, q_rows, PAD), BF),
            pltpu.VMEM((q_heads, q_rows, PAD), BF),
            pltpu.VMEM((kv_heads, k_rows, PAD), BF),
            pltpu.VMEM((kv_heads, PAD, k_rows), BF),
            pltpu.VMEM((kv_heads, k_rows, PAD), BF),
            pltpu.VMEM((k_rows, q_rows), F32),
            pltpu.VMEM((q_rows, q_heads * PAD), BF),
            pltpu.VMEM((kv_heads, k_rows, PAD), F32),
            pltpu.VMEM((kv_heads, k_rows, PAD), F32),
        ],
        compiler_params=pltpu.CompilerParams(vmem_limit_bytes=VMEM_LIMIT),
        cost_estimate=pl.CostEstimate(
            flops=3 * flops, bytes_accessed=8 * seqs * (q_rows * qw + k_rows * kw), transcendentals=0
        ),
        name="attend_back",
    )(*qs, *dos, *kvs, codes_k, codes_q, floor_q, sel_q, sel_kv, lse, *tables)


def rms_factor(values):
    return lax.rsqrt(jnp.mean(values * values, axis=-1, keepdims=True) + EPSILON)


def rms_back(grad_norm, normed, factor):
    inner = jnp.mean(grad_norm * normed, axis=-1, keepdims=True)
    return factor * (grad_norm - normed * inner)


def mm(a, b, ca=1, cb=0):
    return lax.dot_general(a, b, (((ca,), (cb,)), ((), ())), preferred_element_type=F32)


def on_device(
    hidden_in,
    doc_ids,
    span_order,
    norm1_gain,
    w_query,
    w_key,
    w_value,
    w_out,
    norm2_gain,
    w_gate,
    w_up,
    w_down,
    out_cotangent,
):
    seqs, rows, model = hidden_in.shape
    n_dp, n_cp, n_sp = (lax.axis_size(a) for a in ("dp", "cp", "sp"))
    dp, cp, sp = (lax.axis_index(a) for a in ("dp", "cp", "sp"))
    tokens = seqs * rows
    q_heads = w_query.shape[1] // HEAD_DIM // n_sp
    kv_heads = w_key.shape[1] // HEAD_DIM // n_sp
    q_w, kv_w = q_heads * HEAD_DIM, kv_heads * HEAD_DIM
    length = rows * n_sp * n_cp
    span_rows = rows * n_sp // 2
    ff = w_gate.shape[1]
    x_bits = [b for b in bits_of(n_dp) if b > 1]
    y_bits = bits_of(n_cp)
    key_len = len(x_bits) + 1 + len(y_bits)
    core_pos = len(x_bits)
    x_at = [("dp", b, i) for i, b in enumerate(x_bits)]
    y_at = [("cp", b, core_pos + 1 + i) for i, b in enumerate(y_bits)]
    core_at = ("dp", 1, core_pos)
    shape_all = (2,) * key_len

    def gather_rows(value, order):
        pieces = {(0,) * key_len: value}
        for axis, bit, pos in order:
            pieces = gather_bit(pieces, axis, bit, pos)
        return join_rows(pieces)

    def reduce_rows(value, order):
        pieces = split_rows(value, shape_all)
        for axis, bit, pos in order:
            pieces = reduce_bit(pieces, axis, bit, pos)
        return join_rows(pieces)

    order_rel = [(d, r) for d in range(n_cp) for r in range(n_sp)]
    lane = np.arange(PAD) % (PAD // 2)
    freq = np.where(
        lane < HALF, np.float32(ROPE_BASE) ** (-(lane.astype(np.float32) * 2.0 / HEAD_DIM)), 0.0
    ).astype(np.float32)
    sign = np.where(np.arange(PAD) < PAD // 2, -1.0, 1.0).astype(np.float32)

    def positions(d, r):
        stored = ((cp ^ d) * n_sp + (sp - r) % n_sp) * rows
        span = stored // span_rows
        start = jnp.sum(jnp.where(jnp.arange(span_order.shape[0]) == span, span_order, 0)) * span_rows
        return start + stored % span_rows + jnp.arange(rows, dtype=jnp.int32)

    pos = jnp.stack([positions(d, r) for d, r in order_rel])
    angles = pos.reshape(-1).astype(F32)[:, None] * freq[None, :]
    cos_k, sin_k = jnp.cos(angles), jnp.sin(angles) * sign[None, :]
    q_rows = n_sp * rows
    cos_q, sin_q = cos_k[:q_rows].T, -sin_k[:q_rows].T

    docs = [doc_ids] + [shift(doc_ids, "sp", r) for r in range(1, n_sp)]
    docs = jnp.stack(docs, axis=1).reshape(seqs, q_rows)
    docs = jnp.concatenate([docs] + [flip(docs, "cp", d) for d in range(1, n_cp)], axis=1)
    floor = (docs * length).astype(F32)[:, None, :]
    codes = (docs * length + pos.reshape(1, -1)).astype(F32)[:, None, :]
    codes_q, floor_q = codes[:, :, :q_rows], floor[:, :, :q_rows]

    x_input = hidden_in.reshape(tokens, model).astype(F32)
    factor_one = rms_factor(x_input)
    n_one = (x_input * factor_one).astype(BF)
    gain_one = norm1_gain.astype(F32)[:, None]
    gain_two = norm2_gain.astype(F32)[:, None]
    take = lambda w, width: lax.dynamic_slice_in_dim(w, sp * width, width, axis=1)
    qkv_own = jnp.concatenate([take(w_query, q_w), take(w_key, kv_w), take(w_value, kv_w)], axis=1)
    qkv_own = (qkv_own.astype(F32) * gain_one).astype(BF)
    qkv_w = gather_rows(qkv_own, y_at + x_at + [core_at])
    sel_q = jnp.asarray(spread_matrix(q_heads), BF)
    sel_kv = jnp.asarray(spread_matrix(2 * kv_heads), BF)
    w_pad = jnp.concatenate([mm(qkv_w[:, :q_w], sel_q), mm(qkv_w[:, q_w:], sel_kv)], axis=1).astype(BF)

    blocks = [n_one]
    for r in range(1, n_sp):
        blocks.append(shift(blocks[-1], "sp", 1))
    qs, kvs = [], []
    for r in range(n_sp):
        span = slice(r * rows, (r + 1) * rows)
        q, kv = project(blocks[r], w_pad, cos_k[span], sin_k[span], sel_q, sel_kv, seqs, q_heads, kv_heads)
        qs.append(q)
        kvs.append(kv)
    kv_all = kvs + [flip(kv, "cp", d) for d in range(1, n_cp) for kv in kvs]
    heads = (seqs, q_heads, kv_heads)
    *outs, lse = attend(qs, kv_all, codes, codes_q, floor_q, sel_q, sel_kv, *heads)

    out_w = gather_rows(w_out, y_at + x_at + [core_at])
    back = [outs[0]] + [shift(outs[r], "sp", -r) for r in range(1, n_sp)]
    attn = cat([pick(back, (g - sp) % n_sp) for g in range(n_sp)], 1)
    middle = x_input + mm(attn, out_w)
    factor_two = rms_factor(middle)
    normed_two = middle * factor_two
    n_two = normed_two.astype(BF)

    fb = ff // (n_dp * n_cp)

    def reshard(w):
        scaled = (w.astype(F32) * gain_two).astype(BF)
        none = (0,) * key_len
        grid = {(none, c): scaled[:, i * fb : (i + 1) * fb] for i, c in enumerate(np.ndindex(*shape_all))}
        for axis, bit, at in [core_at] + y_at:
            grid = swap_bit(grid, axis, bit, at, at)
        rks, cks = sorted({r for r, _ in grid}), sorted({c for _, c in grid})
        pieces = {r: cat([grid[r, c] for c in cks], 1) for r in rks}
        for axis, bit, at in x_at:
            pieces = gather_bit(pieces, axis, bit, at)
        return join_rows(pieces)

    gate_w, up_w = reshard(w_gate), reshard(w_up)
    down_w = gather_rows(w_down, x_at)
    grad_out = out_cotangent.reshape(tokens, model)

    def tp_rows(value):
        out = []
        for d in range(n_cp):
            v = value if d == 0 else flip(value, "cp", d)
            out.append(jnp.concatenate([v, flip(v, "dp", 1)], axis=0))
        return out

    n_halves, g_halves = tp_rows(n_two), tp_rows(grad_out)
    f_all, dg_all, du_all, ff_parts, dn_parts = [], [], [], [], []

    def to_owner(part, d):
        mine = part[:tokens].astype(F32) + flip(part[tokens:].astype(BF), "dp", 1).astype(F32)
        return mine if d == 0 else flip(mine.astype(BF), "cp", d).astype(F32)

    for d in range(n_cp):
        gate = mm(n_halves[d], gate_w)
        up = mm(n_halves[d], up_w)
        d_hidden_ff = mm(g_halves[d], down_w, 1, 1)
        sig = jax.nn.sigmoid(gate)
        f = (gate * sig * up).astype(BF)
        dg = (d_hidden_ff * up * sig * (1.0 + gate * (1.0 - sig))).astype(BF)
        du = (d_hidden_ff * gate * sig).astype(BF)
        dn_parts.append(to_owner(mm(dg, gate_w, 1, 1) + mm(du, up_w, 1, 1), d))
        ff_parts.append(to_owner(mm(f, down_w), d))
        f_all.append(f)
        dg_all.append(dg)
        du_all.append(du)
    output = middle
    for part in ff_parts:
        output = output + part
    output = output.astype(BF).reshape(seqs, rows, model)
    d_norm_two = dn_parts[0]
    for part in dn_parts[1:]:
        d_norm_two = d_norm_two + part
    d_middle = grad_out.astype(F32) + rms_back(d_norm_two, normed_two, factor_two)
    d_branch = d_middle.astype(BF)

    d_attn = mm(d_branch, out_w, 1, 1).astype(BF)
    groups = [d_attn[:, g * q_w : (g + 1) * q_w] for g in range(n_sp)]
    dos = [pick(groups, (sp + r) % n_sp) for r in range(n_sp)]
    dos = [dos[0]] + [shift(dos[r], "sp", r) for r in range(1, n_sp)]
    tables = (cos_q, sin_q, cos_k, sin_k)
    grads = attend_back(qs, dos, kv_all, codes, codes_q, floor_q, sel_q, sel_kv, lse, tables, *heads)
    dqs, dkvs = grads[:n_sp], grads[n_sp:]
    dqkv = []
    for r in range(n_sp):
        total = dkvs[r].astype(F32)
        for d in range(1, n_cp):
            total = total + flip(dkvs[d * n_sp + r], "cp", d).astype(F32)
        dqkv.append(jnp.concatenate([dqs[r], total.astype(BF)], axis=1))
    moving = None
    for r in list(range(1, n_sp)) + [0]:
        part = mm(dqkv[r], qkv_w, 1, 1)
        if moving is not None:
            part = part + shift(moving.astype(BF), "sp", 1).astype(F32)
        moving = part
    d_input = d_middle + rms_back(moving, x_input * factor_one, factor_one)
    d_input = d_input.astype(BF).reshape(seqs, rows, model)

    d_down = mm(cat(f_all, 0), cat(g_halves, 0), 0, 0)
    x_keys = (2,) * len(x_bits)
    pieces = split_rows(d_down, x_keys)
    for axis, bit, at in x_at:
        pieces = reduce_bit(pieces, axis, bit, at)
    d_down = sum_sp(join_rows(pieces))

    def spread_back(grad):
        pieces = split_rows(grad, shape_all)
        for axis, bit, at in x_at:
            pieces = reduce_bit(pieces, axis, bit, at)
        cols = sorted(np.ndindex(*x_keys))
        rest = (0,) * (key_len - len(x_bits))
        grid = {
            (r, c + rest): v[:, i * fb : (i + 1) * fb].astype(BF) for r, v in pieces.items() for i, c in enumerate(cols)
        }
        for axis, bit, at in reversed([core_at] + y_at):
            grid = unswap_bit(grid, axis, bit, at, at)
        return sum_sp(cat([grid[k] for k in sorted(grid)], 1))

    n_cat = cat(n_halves, 0)
    d_gate = spread_back(mm(n_cat, cat(dg_all, 0), 0, 0))
    d_up = spread_back(mm(n_cat, cat(du_all, 0), 0, 0))
    d_gain_two = jnp.sum(w_gate.astype(F32) * d_gate + w_up.astype(F32) * d_up, axis=1)
    d_out = sum_sp(reduce_rows(mm(attn, d_branch, 0, 0), [core_at] + x_at + y_at))

    d_qkv = mm(cat(blocks, 0), cat(dqkv, 0), 0, 0)
    d_qkv = reduce_rows(d_qkv, [core_at] + x_at + y_at).astype(BF)
    ring = [d_qkv]
    for r in range(1, n_sp):
        ring.append(shift(ring[-1], "sp", 1))
    full = [pick(ring, (sp - g) % n_sp).astype(F32) for g in range(n_sp)]
    d_query = jnp.concatenate([f[:, :q_w] for f in full], axis=1)
    d_key = jnp.concatenate([f[:, q_w : q_w + kv_w] for f in full], axis=1)
    d_value = jnp.concatenate([f[:, q_w + kv_w :] for f in full], axis=1)
    d_gain_one = (
        jnp.sum(w_query.astype(F32) * d_query, axis=1)
        + jnp.sum(w_key.astype(F32) * d_key, axis=1)
        + jnp.sum(w_value.astype(F32) * d_value, axis=1)
    )
    return (
        output,
        d_input,
        d_gain_one,
        d_query * gain_one,
        d_key * gain_one,
        d_value * gain_one,
        d_out,
        d_gain_two,
        d_gate * gain_two,
        d_up * gain_two,
        d_down,
    )


def solution(mesh):
    rows = P(("dp", "cp"), None)
    gain = P(("dp", "cp"))
    token = P("dp", ("cp", "sp"), None)
    placed = (token, P("dp", ("cp", "sp")), P(), gain, rows, rows, rows, rows, gain, rows, rows, rows, token)
    return jax.shard_map(
        on_device,
        mesh=mesh,
        in_specs=placed,
        out_specs=(token, token, gain, rows, rows, rows, rows, gain, rows, rows, rows),
        check_vma=False,
    )
```
